32 devices in a mesh: segment: 4 (over z), mp: 4 (over y, core), tok: 2 (over x).
Axes of the slice: x: 2, y: 2, z: 4, core: 2. Of those that a mesh axis runs over, the one named last changes fastest.
Arguments:
- weights_in: bfloat16 [4, 2, 512, 32768], P('segment', None, None, 'mp'), may hold values from -0.25 to 0.25
- weights_out: bfloat16 [4, 2, 32768, 512], P('segment', None, 'mp'), may hold values from -0.03125 to 0.03125
- norm_gains: float32 [4, 2, 512], P('segment'), may hold values from 0.5 to 1.5
- activations: bfloat16 [4, 2, 2, 256, 512], P('segment', None, 'tok', 'mp'), may hold values from -6 to 6
- gradients: bfloat16 [4, 2, 2, 256, 512], P('segment', None, 'tok', 'mp'), may hold values from -6 to 6
- fresh_inputs: bfloat16 [1, 2, 256, 512], P(None, 'tok', 'mp'), may hold values from -6 to 6
- fresh_gradients: bfloat16 [1, 2, 256, 512], P(None, 'tok', 'mp'), may hold values from -6 to 6
- stashed_inputs: bfloat16 [2, 4, 2, 2, 256, 512], P(None, 'segment', None, 'tok', 'mp'), may hold values from -6 to 6
- stashed_preact: bfloat16 [2, 4, 2, 2, 256, 32768], P(None, 'segment', None, 'tok', None, 'mp'), may hold values from -6 to 6
Outputs:
- leaving_acts: bfloat16 [2, 4, 2, 2, 256, 512], P(None, 'segment', None, 'tok', 'mp')
- leaving_grads: bfloat16 [2, 4, 2, 2, 256, 512], P(None, 'segment', None, 'tok', 'mp')
The draws below stay inside these ranges and needn't reach their ends.
All inputs are finite; a program needn't handle non-finite values.
Results may differ from the reference program's by a relative error of at most 0.014.
Values may be sent and summed in bfloat16 or wider, within the bound.
A program may use at most 128 MiB of HBM per device.

```python
import jax
import jax.numpy as jnp
from jax import lax

D = 512
FF = 32768
TOK_DEV = 256
TICKS = 2
SEGMENTS = 4
HALVES = 2


def levels(stream_key, dims, cuts, smallest, top_value):
    gain = 1.0
    for position, blocks in cuts:
        heights = jax.random.uniform(jax.random.fold_in(jax.random.fold_in(stream_key, 6), position), (blocks,), jnp.float32, smallest / len(cuts), top_value / len(cuts))
        gain = gain * jnp.repeat(jnp.exp(heights), dims[position] // blocks).reshape((-1,) + (1,) * (len(dims) - 1 - position))
    return gain


def bell_draw(own_key, extent, scale, most, cuts=(), held_as=jnp.bfloat16):
    gain = levels(own_key, extent, cuts, -0.22, 0.18) if cuts else 1.0
    values = jax.random.normal(own_key, extent, jnp.float32) * scale * gain
    return jnp.minimum(jnp.maximum(values, -most), most).astype(held_as)


def setup_inputs(seed: int = 0) -> dict:
    key_list = jax.random.split(jax.random.key(seed), 10)
    return {
        "weights_in": bell_draw(key_list[0], (SEGMENTS, 2, D, FF), D ** -0.5, 0.25, ((0, 4), (3, 4))),
        "weights_out": bell_draw(key_list[1], (SEGMENTS, 2, FF, D), FF ** -0.5, 0.03125, ((0, 4), (2, 4))),
        "norm_gains": jnp.clip(0.5 + 1.0 * jax.random.uniform(key_list[2], (SEGMENTS, 2, D), jnp.float32) ** levels(key_list[2], (SEGMENTS, 2, D), ((0, 4),), -0.2, 0.2), 0.5, 1.5),
        "activations": bell_draw(key_list[3], (SEGMENTS, 2, HALVES, TOK_DEV, D), 1.0, 6.0, ((0, 4), (2, 2), (3, 4))),
        "gradients": bell_draw(key_list[4], (SEGMENTS, 2, HALVES, TOK_DEV, D), 1.0, 6.0, ((0, 4), (2, 2), (3, 4))),
        "fresh_inputs": bell_draw(key_list[5], (TICKS - 1, HALVES, TOK_DEV, D), 1.0, 6.0, ((1, 2), (2, 4))),
        "fresh_gradients": bell_draw(key_list[6], (TICKS - 1, HALVES, TOK_DEV, D), 1.0, 6.0, ((1, 2), (2, 4))),
        "stashed_inputs": bell_draw(key_list[7], (TICKS, SEGMENTS, 2, HALVES, TOK_DEV, D), 1.0, 6.0, ((1, 4), (3, 2), (4, 4))),
        "stashed_preact": bell_draw(key_list[8], (TICKS, SEGMENTS, 2, HALVES, TOK_DEV, FF), 1.0, 6.0, ((1, 4), (3, 2), (5, 4))),
    }


epsilon = 1e-06

def normalize(values, gain_row):
    values_wide = values.astype(jnp.float32)
    inverse = lax.rsqrt(lax.optimization_barrier(jnp.mean(values_wide * values_wide, axis=-1, keepdims=True)) + epsilon)
    return values_wide * inverse * gain_row

def forward_layer(rows, gain_row, weight_in, weight_out):
    flat = rows.reshape(-1, rows.shape[-1])
    normed = normalize(flat, gain_row).astype(jnp.bfloat16)
    hidden = jax.nn.relu(jnp.dot(normed, weight_in, preferred_element_type=jnp.float32)).astype(jnp.bfloat16)
    summed = flat.astype(jnp.float32) + jnp.dot(hidden, weight_out, preferred_element_type=jnp.float32)
    return summed.astype(jnp.bfloat16).reshape(rows.shape)

def norm_backward(gradient, stashed, gain_row, norm_grad):
    stashed_wide = stashed.astype(jnp.float32)
    inverse = lax.rsqrt(lax.optimization_barrier(jnp.mean(stashed_wide * stashed_wide, axis=-1, keepdims=True)) + epsilon)
    scaled = gain_row * norm_grad
    inner_sum = lax.optimization_barrier(jnp.mean(stashed_wide * scaled, axis=-1, keepdims=True))
    result = gradient.astype(jnp.float32) + inverse * scaled - stashed_wide * inverse * inverse * inverse * inner_sum
    return result.astype(jnp.bfloat16)

def backward_layer(gradient, stashed, stash_pre, gain_row, weight_in, weight_out):
    flat_grad = gradient.reshape(-1, gradient.shape[-1])
    flat_stash = stashed.reshape(-1, stashed.shape[-1])
    flat_pre = stash_pre.reshape(-1, stash_pre.shape[-1])
    upward = jnp.dot(flat_grad, weight_out.T, preferred_element_type=jnp.float32)
    masked = jnp.where(flat_pre > 0, upward, jnp.zeros_like(upward)).astype(jnp.bfloat16)
    norm_grad = jnp.dot(masked, weight_in.T, preferred_element_type=jnp.float32)
    return norm_backward(flat_grad, flat_stash, gain_row, norm_grad).reshape(gradient.shape)

def reference(weights_in, weights_out, norm_gains, activations, gradients, fresh_inputs, fresh_gradients, stashed_inputs, stashed_preact):
    acts_now = activations
    grads_now = gradients
    forward_ticks = []
    backward_ticks = []
    for tick_index in range(TICKS):
        forward_rows = []
        backward_rows = []
        for section in range(SEGMENTS):
            forward_legs = []
            backward_legs = []
            for leg_index in range(2):
                forward_legs.append(forward_layer(acts_now[section, leg_index], norm_gains[section, leg_index], weights_in[section, leg_index], weights_out[section, leg_index]))
                backward_legs.append(backward_layer(grads_now[section, leg_index], stashed_inputs[tick_index, section, leg_index], stashed_preact[tick_index, section, leg_index], norm_gains[section, leg_index], weights_in[section, leg_index], weights_out[section, leg_index]))
            forward_rows.append(jnp.stack(forward_legs))
            backward_rows.append(jnp.stack(backward_legs))
        forward_all = jnp.stack(forward_rows)
        backward_all = jnp.stack(backward_rows)
        forward_ticks.append(forward_all)
        backward_ticks.append(backward_all)
        if tick_index + 1 < TICKS:
            descent = jnp.concatenate([fresh_inputs[tick_index][None], forward_all[:-1, 0]], axis=0)
            ascent = jnp.concatenate([forward_all[1:, 1], forward_all[-1:, 0]], axis=0)
            acts_now = jnp.stack([descent, ascent], axis=1)
            grad_ascent = jnp.concatenate([fresh_gradients[tick_index][None], backward_all[:-1, 1]], axis=0)
            grad_descent = jnp.concatenate([backward_all[1:, 0], backward_all[-1:, 1]], axis=0)
            grads_now = jnp.stack([grad_descent, grad_ascent], axis=1)
    return (jnp.stack(forward_ticks), jnp.stack(backward_ticks))
```

```python
import functools

import jax
import jax.numpy as jnp
from jax import lax
from jax.experimental import pallas as pl
from jax.experimental.pallas import tpu as pltpu
from jax.sharding import PartitionSpec as P

MESH = pl.DeviceIdType.MESH
EPS = 1e-06
QUARTERS = 4
ORDER = ((True, 0), (False, 0), (False, 1), (True, 1))
F0, B0, B1, F1 = range(4)


def normalize(values, gain_row):
    wide = values.astype(jnp.float32)
    inverse = lax.rsqrt(jnp.mean(wide * wide, axis=-1, keepdims=True) + EPS)
    return (wide * inverse * gain_row).astype(jnp.bfloat16)


def norm_backward(gradient, stashed, gain_row, norm_grad):
    wide = stashed.astype(jnp.float32)
    inverse = lax.rsqrt(jnp.mean(wide * wide, axis=-1, keepdims=True) + EPS)
    scaled = gain_row * norm_grad
    inner = jnp.mean(wide * scaled, axis=-1, keepdims=True)
    result = gradient.astype(jnp.float32) + inverse * scaled - wide * (inverse * inverse * inverse * inner)
    return result.astype(jnp.bfloat16)


def kernel(
    n, sections, ticks,
    w_in_hbm, w_out_hbm, gains_hbm, acts_hbm, grads_hbm, fresh_a_hbm, fresh_g_hbm, stash_hbm, pre_hbm,
    out_a_hbm, out_g_hbm,
    w_in, w_out, pre, gains, rows_in, fresh, stash,
    gather, acc, own, s1_send, s1_recv, s2_send, s2_recv, outs, hop,
    w_sem, pre_sem, small_sem, far_ssem, far_rsem, near_ssem, near_rsem, s1_ssem, s1_rsem, s2_ssem, s2_rsem, hop_ssem, hop_rsem, out_sem,
):
    me = lax.axis_index("mp")
    seg = lax.axis_index("segment")
    core = lax.rem(me, 2)
    chip = me // 2
    chips = n // 2
    partner = chip * 2 + (1 - core)
    is_first = seg == 0
    is_last = seg == sections - 1
    r = rows_in.shape[2]
    quarter = w_in.shape[2] // QUARTERS
    near_rows = slice(0, 2 * r)
    far_rows = slice(2 * r, n * r)

    def rows(k, which):
        return pl.ds(pl.multiple_of((2 * k + which) * r, r), r)

    small = [
        pltpu.make_async_copy(acts_hbm, rows_in.at[0], small_sem.at[0]),
        pltpu.make_async_copy(gains_hbm, gains, small_sem.at[1]),
        pltpu.make_async_copy(grads_hbm, rows_in.at[1], small_sem.at[2]),
        pltpu.make_async_copy(stash_hbm, stash, small_sem.at[3]),
        pltpu.make_async_copy(fresh_a_hbm, fresh.at[0], small_sem.at[4]),
        pltpu.make_async_copy(fresh_g_hbm, fresh.at[1], small_sem.at[5]),
    ]

    def w_copies(leg, i):
        cut = pl.ds(i * quarter, quarter)
        return (
            pltpu.make_async_copy(w_in_hbm.at[leg, :, cut], w_in.at[leg, :, cut], w_sem.at[0, leg, i]),
            pltpu.make_async_copy(w_out_hbm.at[leg, cut, :], w_out.at[leg, cut, :], w_sem.at[1, leg, i]),
        )

    def pre_copies(t, leg, i):
        cut = pl.ds(i * quarter, quarter)
        return [
            pltpu.make_async_copy(
                pre_hbm.at[t, leg, pl.ds(pl.multiple_of(lax.rem(chip + k, chips) * 2 * r, 2 * r), 2 * r), cut],
                pre.at[2 * t + leg, pl.ds(2 * k * r, 2 * r), cut],
                pre_sem.at[2 * t + leg, i, k],
            )
            for k in range(chips)
        ]

    small[0].start()
    small[1].start()
    small[2].start()
    for i in range(QUARTERS):
        for copy in w_copies(0, i):
            copy.start()
    for copy in small[3:]:
        copy.start()

    barrier = pltpu.get_barrier_semaphore()
    for d in range(1, n):
        pl.semaphore_signal(barrier, inc=1, device_id={"mp": lax.rem(me + d, n)}, device_id_type=MESH)

    @pl.when(seg > 0)
    def _():
        pl.semaphore_signal(barrier, inc=1, device_id={"segment": seg - 1}, device_id_type=MESH)

    @pl.when(seg < sections - 1)
    def _():
        pl.semaphore_signal(barrier, inc=1, device_id={"segment": seg + 1}, device_id_type=MESH)

    peers = n - 1 + (seg > 0).astype(jnp.int32) + (seg < sections - 1).astype(jnp.int32)
    pl.semaphore_wait(barrier, peers)

    def far_copy(p, d):
        return pltpu.make_async_remote_copy(
            src_ref=gather.at[p, rows(0, core)], dst_ref=gather.at[p, rows(chips - d, core)],
            send_sem=far_ssem.at[p, d - 1], recv_sem=far_rsem.at[p, d - 1],
            device_id={"mp": lax.rem(chip + d, chips) * 2 + core}, device_id_type=MESH,
        )

    def near_copy(p, k):
        return pltpu.make_async_remote_copy(
            src_ref=gather.at[p, rows(k, core)], dst_ref=gather.at[p, rows(k, core)],
            send_sem=near_ssem.at[p, k], recv_sem=near_rsem.at[p, k],
            device_id={"mp": partner}, device_id_type=MESH,
        )

    def s1_copy(p, part):
        cut = pl.ds(0, 1) if part == 0 else pl.ds(1, chips - 1)
        return pltpu.make_async_remote_copy(
            src_ref=s1_send.at[p, cut], dst_ref=s1_recv.at[p, cut],
            send_sem=s1_ssem.at[p, part], recv_sem=s1_rsem.at[p, part],
            device_id={"mp": partner}, device_id_type=MESH,
        )

    def s2_copy(p, d):
        return pltpu.make_async_remote_copy(
            src_ref=s2_send.at[p, d - 1], dst_ref=s2_recv.at[p, d - 1],
            send_sem=s2_ssem.at[p, d - 1], recv_sem=s2_rsem.at[p, d - 1],
            device_id={"mp": lax.rem(chip + d, chips) * 2 + core}, device_id_type=MESH,
        )

    def hop_copy(t, kind):
        p = 4 * t + kind
        step = 1 if kind in (F0, B1) else -1
        return pltpu.make_async_remote_copy(
            src_ref=outs.at[p], dst_ref=hop.at[p],
            send_sem=hop_ssem.at[p], recv_sem=hop_rsem.at[p],
            device_id={"segment": seg + step}, device_id_type=MESH,
        )

    def hop_sends(kind):
        return jnp.logical_not(is_last) if kind in (F0, B1) else jnp.logical_not(is_first)

    def hop_arrives(kind):
        return jnp.logical_not(is_first) if kind in (F0, B1) else jnp.logical_not(is_last)

    def out_copy(t, kind):
        forward, leg = ORDER[kind]
        p = 4 * t + kind
        return pltpu.make_async_copy(
            outs.at[p], (out_a_hbm if forward else out_g_hbm).at[t, leg], out_sem.at[p]
        )

    def rows_ref(t, kind):
        forward, leg = ORDER[kind]
        return rows_in.at[2 * t + (0 if forward else 1), leg]

    def enter(t, kind):
        forward, leg = ORDER[kind]
        p = 4 * t + kind
        values = rows_ref(t, kind)[...]
        gather[p, rows(0, core)] = normalize(values, gains[pl.ds(leg, 1), :]) if forward else values
        for d in range(1, chips):
            far_copy(p, d).start()
        near_copy(p, 0).start()

    def relay(t, kind):
        p = 4 * t + kind
        for d in range(1, chips):
            far_copy(p, d).wait_recv()
            near_copy(p, chips - d).start()

    def arrive(t, kind):
        target = rows_ref(t, kind)
        before = 4 * t - 4

        @pl.when(hop_arrives(kind))
        def _():
            hop_copy(t - 1, kind).wait_recv()
            target[...] = hop[before + kind]

        @pl.when(jnp.logical_not(hop_arrives(kind)))
        def _():
            if kind == F0:
                target[...] = fresh[0, t - 1]
            elif kind == B1:
                target[...] = fresh[1, t - 1]
            elif kind == F1:
                target[...] = outs[before + F0]
            else:
                target[...] = outs[before + B1]

        enter(t, kind)

    def scatter_one(t, kind, part):
        p = 4 * t + kind
        for k in range(1) if part == 0 else range(1, chips):
            s1_send[p, k] = acc[kind % 2, rows(k, 1 - core)].astype(jnp.bfloat16)
        s1_copy(p, part).start()

    def scatter_far(t, kind):
        p = 4 * t + kind
        s1_copy(p, 1).wait_recv()
        for d in range(1, chips):
            s2_send[p, d - 1] = (
                acc[kind % 2, rows(d, core)] + s1_recv[p, d].astype(jnp.float32)
            ).astype(jnp.bfloat16)
            s2_copy(p, d).start()

    def scatter_own(t, kind):
        p = 4 * t + kind
        s1_copy(p, 0).wait_recv()
        own[p] = acc[kind % 2, rows(0, core)] + s1_recv[p, 0].astype(jnp.float32)

    def scatter_two(t, kind):
        scatter_far(t, kind)
        scatter_own(t, kind)

    def finish(t, kind):
        forward, leg = ORDER[kind]
        p = 4 * t + kind
        total = own[p]
        for d in range(1, chips):
            s2_copy(p, d).wait_recv()
            total = total + s2_recv[p, d - 1].astype(jnp.float32)
        entered = rows_ref(t, kind)[...]
        if forward:
            outs[p] = (entered.astype(jnp.float32) + total).astype(jnp.bfloat16)
        else:
            outs[p] = norm_backward(entered, stash[t, leg], gains[pl.ds(leg, 1), :], total)
        out_copy(t, kind).start()

        @pl.when(jnp.logical_and(t + 1 < ticks, hop_sends(kind)))
        def _():
            hop_copy(t, kind).start()

    def first(t, call):
        pl.when(t == 0)(lambda: (call(), None)[1])

    def later(t, call):
        pl.when(t > 0)(lambda: (call(), None)[1])

    def more(t, call):
        pl.when(t + 1 < ticks)(lambda: (call(), None)[1])

    def near_ready(t, kind):
        near_copy(4 * t + kind, 0).wait_recv()

    def far_ready(t, kind):
        for d in range(1, chips):
            near_copy(4 * t + kind, chips - d).wait_recv()

    def load_rest():
        for i in range(QUARTERS):
            for copy in pre_copies(0, 0, i):
                copy.start()
        for i in range(QUARTERS):
            for copy in pre_copies(0, 1, i):
                copy.start()
            for copy in w_copies(1, i):
                copy.start()

    def load_next(t):
        for leg in range(2):
            for i in range(QUARTERS):
                for copy in pre_copies(t + 1, leg, i):
                    copy.start()

    def wait_w(leg, i):
        for copy in w_copies(leg, i):
            copy.wait()

    def wait_pre(t, leg, i):
        for copy in pre_copies(t, leg, i):
            copy.wait()

    def wait_small():
        for copy in small[3:]:
            copy.wait()

    def forward_step(t, kind, part, i):
        leg = ORDER[kind][1]
        cut = slice(i * quarter, (i + 1) * quarter)
        x = gather[4 * t + kind, part]
        hidden = jnp.maximum(jnp.dot(x, w_in[leg, :, cut], preferred_element_type=jnp.float32), 0.0)
        added = jnp.dot(hidden.astype(jnp.bfloat16), w_out[leg, cut, :], preferred_element_type=jnp.float32)
        if i == 0:
            acc[kind % 2, part] = added
        else:
            acc[kind % 2, part] += added

    def backward_step(t, kind, i):
        leg = ORDER[kind][1]
        cut = slice(i * quarter, (i + 1) * quarter)
        x = gather[4 * t + kind]
        up = lax.dot_general(
            x, w_out[leg, cut, :], (((1,), (1,)), ((), ())), preferred_element_type=jnp.float32
        )
        masked = jnp.where(pre[2 * t + leg, :, cut].astype(jnp.float32) > 0, up, 0.0).astype(jnp.bfloat16)
        added = lax.dot_general(
            masked, w_in[leg, :, cut], (((1,), (1,)), ((), ())), preferred_element_type=jnp.float32
        )
        if i == 0:
            acc[kind % 2] = added
        else:
            acc[kind % 2] += added

    small[0].wait()
    small[1].wait()
    enter(0, F0)
    small[2].wait()
    enter(0, B0)
    load_rest()

    def tick(t, carry):
        later(t, lambda: (finish(t - 1, B1), arrive(t, B0)))
        near_ready(t, F0)
        for i in range(QUARTERS):
            if i == 2:
                later(t, lambda: scatter_own(t - 1, F1))
            if i == 3:
                first(t, lambda: relay(0, F0))
            first(t, lambda: wait_w(0, i))
            forward_step(t, F0, near_rows, i)
        far_ready(t, F0)
        for i in range(QUARTERS):
            if i == 2:
                relay(t, B0)
                first(t, lambda: (wait_small(), enter(0, B1)))
                later(t, lambda: arrive(t, B1))
            forward_step(t, F0, far_rows, i)
        scatter_one(t, F0, 1)
        scatter_one(t, F0, 0)

        near_ready(t, B0)
        far_ready(t, B0)
        for i in range(QUARTERS):
            if i == 0:
                later(t, lambda: finish(t - 1, F1))
            if i == 1:
                scatter_two(t, F0)
            if i == 2:
                relay(t, B1)
            if i == 3:
                first(t, lambda: enter(0, F1))
                later(t, lambda: arrive(t, F1))
            wait_pre(t, 0, i)
            backward_step(t, B0, i)
        scatter_one(t, B0, 1)
        scatter_one(t, B0, 0)

        near_ready(t, B1)
        far_ready(t, B1)
        for i in range(QUARTERS):
            if i == 0:
                finish(t, F0)
            if i == 1:
                scatter_two(t, B0)
            if i == 2:
                relay(t, F1)
            if i == 3:
                more(t, lambda: arrive(t + 1, F0))
            first(t, lambda: wait_w(1, i))
            wait_pre(t, 1, i)
            backward_step(t, B1, i)
        scatter_one(t, B1, 1)
        scatter_one(t, B1, 0)

        near_ready(t, F1)
        far_ready(t, F1)
        for i in range(QUARTERS):
            if i == 0:
                more(t, lambda: load_next(t))
                finish(t, B0)
            if i == 2:
                scatter_two(t, B1)
            forward_step(t, F1, far_rows, i)
        scatter_one(t, F1, 1)
        for i in range(QUARTERS):
            if i == 0:
                more(t, lambda: relay(t + 1, F0))
            if i == 2:
                scatter_far(t, F1)
            forward_step(t, F1, near_rows, i)
        scatter_one(t, F1, 0)
        return carry

    lax.fori_loop(0, ticks, tick, 0)
    finish(ticks - 1, B1)
    scatter_own(ticks - 1, F1)
    finish(ticks - 1, F1)

    def drain(t, carry):
        for kind in range(4):
            p = 4 * t + kind
            for d in range(1, chips):
                far_copy(p, d).wait_send()
            for k in range(chips):
                near_copy(p, k).wait_send()
            s1_copy(p, 0).wait_send()
            s1_copy(p, 1).wait_send()
            for d in range(1, chips):
                s2_copy(p, d).wait_send()

            @pl.when(jnp.logical_and(t + 1 < ticks, hop_sends(kind)))
            def _():
                hop_copy(t, kind).wait_send()

            out_copy(t, kind).wait()
        return carry

    lax.fori_loop(0, ticks, drain, 0)


def flush(a_ref, g_ref, out_a_ref, out_g_ref, held, sem):
    pairs = ((a_ref, out_a_ref), (g_ref, out_g_ref))
    loads = [pltpu.make_async_copy(src, held.at[k], sem.at[0, k]) for k, (src, _) in enumerate(pairs)]
    stores = [pltpu.make_async_copy(held.at[k], dst, sem.at[1, k]) for k, (_, dst) in enumerate(pairs)]
    for copy in loads:
        copy.start()
    for load, store in zip(loads, stores):
        load.wait()
        store.start()
    for copy in stores:
        copy.wait()


def body(n, sections, w_in, w_out, gains, acts, grads, fresh_a, fresh_g, stash, pre):
    ticks = stash.shape[0]
    _, legs, d, ff = w_in.shape
    r = acts.shape[3]
    total_rows = n * r
    chips = n // 2
    passes = 4 * ticks
    bf16, f32 = jnp.bfloat16, jnp.float32
    any_spec = pl.BlockSpec(memory_space=pl.ANY)
    dma = pltpu.SemaphoreType.DMA
    far = max(chips - 1, 1)
    out = jax.ShapeDtypeStruct((ticks, legs, r, d), bf16)
    out_a, out_g = pl.pallas_call(
        functools.partial(kernel, n, sections, ticks),
        out_shape=(out, out),
        in_specs=[any_spec] * 9,
        out_specs=(any_spec, any_spec),
        scratch_shapes=[
            pltpu.VMEM((legs, d, ff), bf16),
            pltpu.VMEM((legs, ff, d), bf16),
            pltpu.VMEM((ticks * legs, total_rows, ff), bf16),
            pltpu.VMEM((legs, d), f32),
            pltpu.VMEM((2 * ticks, legs, r, d), bf16),
            pltpu.VMEM((2,) + (max(ticks - 1, 1), r, d), bf16),
            pltpu.VMEM((ticks, legs, r, d), bf16),
            pltpu.VMEM((passes, total_rows, d), bf16),
            pltpu.VMEM((2, total_rows, d), f32),
            pltpu.VMEM((passes, r, d), f32),
            pltpu.VMEM((passes, chips, r, d), bf16),
            pltpu.VMEM((passes, chips, r, d), bf16),
            pltpu.VMEM((passes, far, r, d), bf16),
            pltpu.VMEM((passes, far, r, d), bf16),
            pltpu.VMEM((passes, r, d), bf16),
            pltpu.VMEM((passes, r, d), bf16),
            dma((2, legs, QUARTERS)),
            dma((ticks * legs, QUARTERS, chips)),
            dma((6,)),
            dma((passes, far)),
            dma((passes, far)),
            dma((passes, chips)),
            dma((passes, chips)),
            dma((passes, 2)),
            dma((passes, 2)),
            dma((passes, far)),
            dma((passes, far)),
            dma((passes,)),
            dma((passes,)),
            dma((passes,)),
        ],
        compiler_params=pltpu.CompilerParams(
            collective_id=0, has_side_effects=True, vmem_limit_bytes=67043328
        ),
        name="relay",
    )(
        w_in[0], w_out[0], gains[0], acts[0, :, 0], grads[0, :, 0],
        fresh_a[:, 0], fresh_g[:, 0], stash[:, 0, :, 0], pre[:, 0, :, 0],
    )
    out_a, out_g = pl.pallas_call(
        flush,
        out_shape=(out, out),
        in_specs=[any_spec] * 2,
        out_specs=(any_spec, any_spec),
        scratch_shapes=[pltpu.VMEM((2,) + out.shape, bf16), dma((2, 2))],
        name="flush",
    )(out_a, out_g)
    return out_a[:, None, :, None], out_g[:, None, :, None]


def solution(mesh):
    return jax.shard_map(
        functools.partial(body, mesh.shape["mp"], mesh.shape["segment"]),
        mesh=mesh,
        in_specs=(
            P("segment", None, None, "mp"),
            P("segment", None, "mp", None),
            P("segment", None, None),
            P("segment", None, "tok", "mp", None),
            P("segment", None, "tok", "mp", None),
            P(None, "tok", "mp", None),
            P(None, "tok", "mp", None),
            P(None, "segment", None, "tok", "mp", None),
            P(None, "segment", None, "tok", None, "mp"),
        ),
        out_specs=(
            P(None, "segment", None, "tok", "mp", None),
            P(None, "segment", None, "tok", "mp", None),
        ),
        check_vma=False,
    )
```
